32 devices in a mesh: groups: 1, seq: 32 (over z, y, x, core).
Axes of the slice: x: 2, y: 2, z: 4, core: 2. Of those that a mesh axis runs over, the one named last changes fastest.
Arguments:
- queries: bfloat16 [8192, 2048], P(('groups', 'seq')), may hold values from -6 to 6
- keys: bfloat16 [8192, 2048], P(('groups', 'seq')), may hold values from -6 to 6
- values: bfloat16 [8192, 2048], P(('groups', 'seq')), may hold values from -6 to 6
- out_weight: bfloat16 [2048, 2048], replicated, may hold values from -0.125 to 0.125
- out_grad: bfloat16 [8192, 2048], P(('groups', 'seq')), may hold values from -6 to 6
Outputs:
- query_grad: bfloat16 [8192, 2048], P(('groups', 'seq'))
- key_grad: bfloat16 [8192, 2048], P(('groups', 'seq'))
- value_grad: bfloat16 [8192, 2048], P(('groups', 'seq'))
- weight_grad: float32 [2048, 2048], P(('groups', 'seq'))
The draws below stay inside these ranges and needn't reach their ends.
All inputs are finite; a program needn't handle non-finite values.
Results may differ from the reference program's by a relative error of at most 0.0033.
Values sent between devices are 32-bit elements; how exact they have to be, the bound alone decides.
A program may use at most 192 MiB of HBM per device.

```python
import jax
import jax.numpy as jnp
from jax import lax

D = 2048
HEADS = 16
HEAD = 128
TOK_DEV = 256
TOKENS = 8192
HD = 2048


def steps_of(own_key, shape, cuts, least, high):
    gain, own = 1.0, jax.random.fold_in(own_key, 6)
    for axis_at, parts in cuts:
        steps = jnp.exp(jax.random.uniform(jax.random.fold_in(own, axis_at), (parts,), jnp.float32, least / len(cuts), high / len(cuts)))
        gain = gain * jnp.repeat(steps, shape[axis_at] // parts).reshape([-1 if axis == axis_at else 1 for axis in range(len(shape))])
    return gain


def scatter_about(key, dims, spread, limit, shards=(), held_as=jnp.bfloat16):
    factor_of = steps_of(key, dims, shards, -0.22, 0.18) if shards else 1.0
    result = jax.random.normal(key, dims, jnp.float32) * spread * factor_of
    return jnp.minimum(jnp.maximum(result, -limit), limit).astype(held_as)


def setup_inputs(seed: int = 0, part: int = 0) -> dict:
    key_list = jax.random.split(jax.random.key(seed), 6)
    part_keys = jax.random.split(jax.random.fold_in(key_list[5], part), 6)
    queries = scatter_about(part_keys[0], (TOKENS, HD), 1.5, 6.0, ((0, 32),))
    keys = scatter_about(part_keys[1], (TOKENS, HD), 1.5, 6.0, ((0, 32),))
    values = scatter_about(part_keys[2], (TOKENS, HD), 1.0, 6.0, ((0, 32),))
    out_weight = scatter_about(key_list[3], (HD, D), HD ** -0.5, 0.125)
    out_grad = scatter_about(part_keys[4], (TOKENS, D), 1.0, 6.0, ((0, 32),))
    return {"queries": queries, "keys": keys, "values": values, "out_weight": out_weight, "out_grad": out_grad}


def feature(x):
    return jax.nn.elu(x) + 1.0

def attend_block(query_f, key_f, value_f, state, zsum):
    block_len = query_f.shape[0]
    fq = feature(query_f.reshape(block_len, HEADS, HEAD))
    fk = feature(key_f.reshape(block_len, HEADS, HEAD))
    vv = value_f.reshape(block_len, HEADS, HEAD)
    rows = lax.broadcasted_iota(jnp.int32, (block_len, block_len), 0)
    cols = lax.broadcasted_iota(jnp.int32, (block_len, block_len), 1)
    causal = (cols <= rows).astype(jnp.float32)
    scores = jnp.einsum('thd,shd->hts', fq, fk, precision=lax.Precision.HIGHEST) * causal[None]
    numer = jnp.einsum('hts,she->the', scores, vv, precision=lax.Precision.HIGHEST)
    numer = numer + jnp.einsum('thd,hde->the', fq, state, precision=lax.Precision.HIGHEST)
    denom = lax.optimization_barrier(jnp.sum(scores, axis=2)).T + jnp.einsum('thd,hd->th', fq, zsum, precision=lax.Precision.HIGHEST)
    return (numer / denom[:, :, None]).reshape(block_len, HEADS * HEAD)

def forward(query_f, key_f, value_f):
    count = TOKENS // TOK_DEV
    qb = query_f.reshape(count, TOK_DEV, HEADS * HEAD)
    kb = key_f.reshape(count, TOK_DEV, HEADS * HEAD)
    vb = value_f.reshape(count, TOK_DEV, HEADS * HEAD)

    def step(carry, pieces):
        state, zsum = carry
        qp, kp, vp = pieces
        out = attend_block(qp, kp, vp, state, zsum)
        fk = feature(kp.reshape(TOK_DEV, HEADS, HEAD))
        vv = vp.reshape(TOK_DEV, HEADS, HEAD)
        state = state + jnp.einsum('thd,the->hde', fk, vv, precision=lax.Precision.HIGHEST)
        zsum = zsum + lax.optimization_barrier(jnp.sum(fk, axis=0))
        return ((state, zsum), out)
    init = (jnp.zeros((HEADS, HEAD, HEAD), jnp.float32), jnp.zeros((HEADS, HEAD), jnp.float32))
    _, outs = lax.scan(step, init, (qb, kb, vb))
    return outs.reshape(TOKENS, HEADS * HEAD)

def reference(queries, keys, values, out_weight, out_grad):
    query_f = queries.astype(jnp.float32)
    key_f = keys.astype(jnp.float32)
    value_f = values.astype(jnp.float32)
    attended, pullback = jax.vjp(forward, query_f, key_f, value_f)
    rounded = attended.astype(jnp.bfloat16)
    attended_grad = jnp.dot(out_grad, out_weight.T, preferred_element_type=jnp.float32)
    weight_grad = jnp.dot(rounded.T, out_grad, preferred_element_type=jnp.float32)
    query_grad, key_grad, value_grad = pullback(attended_grad)
    return (query_grad.astype(jnp.bfloat16), key_grad.astype(jnp.bfloat16), value_grad.astype(jnp.bfloat16), weight_grad)
```

```python
import functools

import jax
import jax.numpy as jnp
from jax import lax
from jax.experimental import pallas as pl
from jax.experimental.pallas import tpu as pltpu
from jax.sharding import PartitionSpec as P

HEAD = 128
MESH = pl.DeviceIdType.MESH
BF = jnp.bfloat16
F32 = jnp.float32
NN = (((1,), (0,)), ((), ()))
NT = (((1,), (1,)), ((), ()))
TN = (((0,), (0,)), ((), ()))
QUARTERS = 4
W_SLOTS = 4
W_ROWS = 256


def dot(a, b, dims):
    return lax.dot_general(a, b, dims, preferred_element_type=F32)


def two(x):
    high = x.astype(BF)
    return high, (x - high.astype(F32)).astype(BF)


def mm(a, b, dims):
    a = (a,) if a.dtype == BF else two(a)
    b = (b,) if b.dtype == BF else two(b)
    total = dot(a[0], b[0], dims)
    if len(a) > 1:
        total += dot(a[1], b[0], dims)
    if len(b) > 1:
        total += dot(a[0], b[1], dims)
    return total


def features(x):
    x = x.astype(F32)
    return jnp.where(x > 0, x + 1.0, jnp.exp(jnp.minimum(x, 0.0)))


def bit_of(x, k):
    return (x // (1 << k)) % 2


def flip(x, mask):
    for k in range(mask.bit_length()):
        if (mask >> k) & 1:
            x = x + (1 - 2 * bit_of(x, k)) * (1 << k)
    return x


def loop(start, stop, unroll, one):
    assert (stop - start) % unroll == 0

    def body(i, carry):
        for j in range(unroll):
            one(start + i * unroll + j)
        return carry

    lax.fori_loop(0, (stop - start) // unroll, body, 0)


def scratch_of(tokens, width, out_width):
    heads, shard = width // HEAD, width // 8
    piece = width // 32 // QUARTERS
    vm = {}
    for name in ("q", "k", "v", "fq", "fk"):
        vm[name] = ((tokens, width), BF)
    vm["og"] = ((tokens, out_width), BF)
    vm["wb"] = ((W_SLOTS, W_ROWS, out_width), BF)
    vm["vt"] = ((width, tokens), BF)
    vm["da"] = ((width, tokens), F32)
    vm["nl"] = ((width, tokens), F32)
    vm["inv"] = ((heads, tokens), F32)
    vm["dd"] = ((heads, tokens), F32)
    for s in ("s", "g"):
        vm[s + "x"] = ((width, HEAD), F32)
        vm[s + "xp"] = ((width, HEAD), F32)
        vm[s + "t"] = ((width // 2, HEAD), F32)
        vm[s + "p"] = ((shard, HEAD), F32)
        for name in ("u", "z", "n"):
            vm[s + name] = ((4, shard, HEAD), F32)
        vm[s + "e"] = ((width, HEAD), F32)
    for s in ("a", "b"):
        vm["v" + s + "b"] = ((8, heads, HEAD), F32)
        vm["v" + s + "p"] = ((heads, HEAD), F32)
        vm["v" + s + "l"] = ((4, heads, HEAD), F32)
        vm["v" + s + "e"] = ((heads, HEAD), F32)
    vm["og32"] = ((tokens, out_width), F32)
    vm["ogr"] = ((3, tokens, out_width), F32)
    vm["ogb"] = ((4 * tokens, out_width), BF)
    vm["at"] = ((2, 2, QUARTERS, 8, piece, tokens), F32)
    vm["ar"] = ((3, QUARTERS, 8, piece, tokens), F32)
    vm["lhs"] = ((8 * piece, 4 * tokens), BF)
    vm["part"] = ((QUARTERS, 2, 2, 2 * piece, out_width), F32)
    vm["r1"] = ((QUARTERS, 2, 2 * piece, out_width), F32)
    vm["r2"] = ((QUARTERS, 2 * piece, out_width), F32)
    vm["r3"] = ((QUARTERS, piece, out_width), F32)
    return vm


COPIES = 96


class Links:
    def __init__(self, me, send, recv):
        self.me, self.send, self.recv, self.used, self.sent = me, send, recv, 0, []

    def copy(self, src, dst, mask, when=None):
        i = self.used
        self.used += 1
        made = pltpu.make_async_remote_copy(
            src_ref=src, dst_ref=dst, send_sem=self.send.at[i], recv_sem=self.recv.at[i],
            device_id={"seq": flip(self.me, mask)}, device_id_type=MESH)
        if when is None:
            made.start()
        else:
            pl.when(when)(made.start)
        self.sent.append((made, when))
        return made

    def drain(self):
        for made, when in self.sent:
            if when is None:
                made.wait_send()
            else:
                pl.when(when)(made.wait_send)


class StateScan:
    def __init__(self, links, r, s, later):
        self.links, self.later = links, later
        self.x, self.xp, self.t, self.p = r[s + "x"], r[s + "xp"], r[s + "t"], r[s + "p"]
        self.u, self.z, self.n, self.e = r[s + "u"], r[s + "z"], r[s + "n"], r[s + "e"]
        me = links.me
        self.core, self.chip, self.layer = me % 2, (me // 2) % 4, me // 8
        self.half = self.x.shape[0] // 2
        self.shard = self.p.shape[0]

    def before(self, a, b):
        return a > b if self.later else a < b

    def rows(self, ref, start, size):
        return ref.at[pl.ds(pl.multiple_of(start, 8), size)]

    def give(self):
        at = (1 - self.core) * self.half
        self.c1 = self.links.copy(self.rows(self.x, at, self.half), self.rows(self.xp, at, self.half), 1)

    def give_rest(self):
        at = self.core * self.half
        self.c2 = self.links.copy(self.rows(self.x, at, self.half), self.rows(self.xp, at, self.half), 1)

    def spread(self):
        self.c1.wait_recv()
        at = pl.ds(pl.multiple_of(self.core * self.half, 8), self.half)
        self.t[...] = self.x[at, :] + self.xp[at, :]
        self.c3 = [
            self.links.copy(self.rows(self.t, flip(self.chip, j) * self.shard, self.shard), self.u.at[j], 2 * j)
            for j in (1, 2, 3)]

    def climb(self):
        self.u[0] = self.t[pl.ds(pl.multiple_of(self.chip * self.shard, 8), self.shard), :]
        for c in self.c3:
            c.wait_recv()
        self.p[...] = (self.u[0] + self.u[1]) + (self.u[2] + self.u[3])
        self.c4 = []
        for j in (1, 2, 3):
            other = flip(self.layer, j)
            self.c4.append((j, other, self.links.copy(self.p, self.z.at[j], 8 * j, self.before(self.layer, other))))

    def settle(self):
        self.n[0] = jnp.zeros(self.p.shape, F32)
        for j, other, c in self.c4:
            @pl.when(self.before(other, self.layer))
            def _():
                c.wait_recv()
                self.n[0] = self.n[0] + self.z[j]
        entry = self.n[0]
        mine = pl.multiple_of(self.core * self.half + self.chip * self.shard, 8)
        self.c5 = []
        for i in (3, 2, 1, 0):
            chip = flip(self.chip, i)
            value = entry
            for j in range(4):
                if j != i:
                    value = value + jnp.where(self.before(flip(self.chip, j), chip), self.u[j], 0.0)
            if i:
                self.n[i] = value
                self.c5.append(self.links.copy(self.n.at[i], self.rows(self.e, mine, self.shard), 2 * i))
            else:
                self.e[pl.ds(mine, self.shard), :] = value

    def join(self):
        for c in self.c5:
            c.wait_recv()
        block = self.rows(self.e, self.core * self.half, self.half)
        self.c6 = self.links.copy(block, block, 1)

    def finish(self):
        self.c6.wait_recv()
        self.c2.wait_recv()

    def entry(self, at):
        return self.e[at, :] + jnp.where(self.before(1 - self.core, self.core), self.xp[at, :], 0.0)


class RowScan:
    def __init__(self, links, r, s, later):
        self.links, self.later = links, later
        self.b, self.p, self.l, self.e = r["v" + s + "b"], r["v" + s + "p"], r["v" + s + "l"], r["v" + s + "e"]

    def before(self, a, b):
        return a > b if self.later else a < b

    def start(self):
        self.c1 = [self.links.copy(self.b.at[0], self.b.at[j], j) for j in range(1, 8)]

    def climb(self):
        for c in self.c1:
            c.wait_recv()
        total = self.b[0]
        for j in range(1, 8):
            total = total + self.b[j]
        self.p[...] = total
        self.c2 = [self.links.copy(self.p, self.l.at[j], 8 * j) for j in (1, 2, 3)]

    def finish(self):
        me = self.links.me
        spot, layer = me % 8, me // 8
        total = jnp.zeros(self.e.shape, F32)
        for j in range(1, 8):
            total = total + jnp.where(self.before(flip(spot, j), spot), self.b[j], 0.0)
        for j in (1, 2, 3):
            self.c2[j - 1].wait_recv()
            total = total + jnp.where(self.before(flip(layer, j), layer), self.l[j], 0.0)
        self.e[...] = total


PEERS = (1, 2, 3, 4, 5, 6, 7, 8, 9, 16, 24)


def kernel(names, q_hbm, k_hbm, v_hbm, w_hbm, og_hbm, dq_ref, dk_ref, dv_ref, wg_ref, *refs):
    r = dict(zip(names, refs))
    load_sem, w_sem, send, recv = refs[len(names):]
    me = lax.axis_index("seq")
    core, b1, b2, b3, b4 = [bit_of(me, k) for k in range(5)]
    tokens, width = r["q"].shape
    out_width = r["og"].shape[1]
    heads = width // HEAD
    piece = r["r3"].shape[1]
    links = Links(me, send, recv)

    loads = {}
    for i, (name, src) in enumerate((("k", k_hbm), ("v", v_hbm), ("og", og_hbm), ("q", q_hbm))):
        loads[name] = pltpu.make_async_copy(src, r[name], load_sem.at[i])
        loads[name].start()

    def w_load(i):
        return pltpu.make_async_copy(
            w_hbm.at[pl.ds(pl.multiple_of(i * W_ROWS, W_ROWS), W_ROWS)], r["wb"].at[i % W_SLOTS], w_sem.at[i % W_SLOTS])

    for i in range(W_SLOTS):
        w_load(i).start()

    barrier = pltpu.get_barrier_semaphore()
    for mask in PEERS:
        pl.semaphore_signal(barrier, inc=1, device_id={"seq": flip(me, mask)}, device_id_type=MESH)

    state = StateScan(links, r, "s", False)
    grad = StateScan(links, r, "g", True)
    zsum = RowScan(links, r, "a", False)
    zgrad = RowScan(links, r, "b", True)

    def columns(h):
        return pl.ds(pl.multiple_of(h * HEAD, HEAD), HEAD)

    def theirs_first(i):
        return (i + (1 - core) * (heads // 2)) % heads

    def causal():
        shape = (tokens, tokens)
        return lax.broadcasted_iota(jnp.int32, shape, 0) <= lax.broadcasted_iota(jnp.int32, shape, 1)

    def sums(i):
        h = theirs_first(i)
        at = columns(h)
        fk = features(r["k"][:, at])
        r["va" + "b"][0, pl.ds(h, 1), :] = jnp.sum(fk, axis=0, keepdims=True)
        r["fk"][:, at] = fk.astype(BF)
        vt = r["v"][:, at].T
        r["vt"][at, :] = vt
        r["sx"][at, :] = mm(vt, fk, NN)

    loads["k"].wait()
    loads["v"].wait()
    loop(0, heads // 2, 2, sums)
    pl.semaphore_wait(barrier, len(PEERS))
    state.give()
    loop(heads // 2, heads, 2, sums)
    zsum.start()
    state.give_rest()

    loads["og"].wait()
    cols = [pl.ds(j * (out_width // 2), out_width // 2) for j in range(2)]
    r["og32"][...] = r["og"][...].astype(F32)
    state.spread()
    og_z = [links.copy(r["og32"].at[:, c], r["ogr"].at[1, :, c], 8) for c in cols]
    og_c = [links.copy(r["og32"].at[:, c], r["ogr"].at[0, :, c], 1) for c in cols]
    og_d = []

    def relay(j):
        og_z[j].wait_recv()
        og_d.append(links.copy(r["ogr"].at[1, :, cols[j]], r["ogr"].at[2, :, cols[j]], 1))

    def project(i):
        w_load(i).wait()
        rows = pl.ds(pl.multiple_of(i * W_ROWS, W_ROWS), W_ROWS)
        r["da"][rows, :] = dot(r["wb"][i % W_SLOTS], r["og"][...], NT)

        @pl.when(i + W_SLOTS < width // W_ROWS)
        def _():
            w_load(i + W_SLOTS).start()

    loop(0, width // W_ROWS, 1, project)
    zsum.climb()
    loads["q"].wait()

    def query_features(h):
        r["fq"][:, columns(h)] = features(r["q"][:, columns(h)]).astype(BF)

    loop(0, heads, 2, query_features)
    state.climb()
    zsum.finish()

    def rows_of(x, count):
        return [jnp.broadcast_to(y, (count, y.shape[1])) for y in two(x)]

    def local(i):
        h = theirs_first(i)
        at = columns(h)
        fq, fk = r["fq"][:, at], r["fk"][:, at]
        scores = jnp.where(causal(), dot(fk, fq, NT), 0.0)
        z = r["vae"][pl.ds(h, 1), :]
        zhigh, zlow = rows_of(z, 16)
        den = jnp.sum(scores, axis=0, keepdims=True) + (dot(zhigh, fq, NT) + dot(zlow, fq, NT))[0:1, :]
        inv = 1.0 / den
        r["inv"][pl.ds(h, 1), :] = inv
        r["nl"][at, :] = mm(r["vt"][at, :], scores, NN)
        dn = r["da"][at, :] * inv
        r["da"][at, :] = dn
        r["gx"][at, :] = mm(dn, features(r["q"][:, at]), NN)

    loop(0, heads // 2, 2, local)
    grad.give()
    loop(heads // 2, heads, 2, local)
    grad.give_rest()
    grad.spread()
    state.settle()
    relay(0)
    grad.climb()
    state.join()
    state.finish()

    group = heads // 4

    def attend(i):
        far = i // (heads // 2)
        within = i % (heads // 2)
        low = b3 * far + (1 - b3) * (1 - far)
        h = (within // group) * (2 * group) + low * group + within % group
        at = columns(h)
        fq = r["fq"][:, at]
        high, rest = two(state.entry(at))
        att = (r["nl"][at, :] + dot(high, fq, NT) + dot(rest, fq, NT)) * r["inv"][pl.ds(h, 1), :]
        slot = bit_of(h, 0) * 4 + bit_of(h, 1) * 2 + bit_of(h, 3)
        for c in range(2):
            for j in range(QUARTERS):
                start = (c * QUARTERS + j) * piece
                r["at"][low, c, j, slot] = att[start:start + piece, :]
        dden = -jnp.sum(r["da"][at, :] * att, axis=0, keepdims=True)
        r["dd"][pl.ds(h, 1), :] = dden
        dhigh, dlow = rows_of(dden, 16)
        r["vbb"][0, pl.ds(h, 1), :] = (dot(dhigh, fq, NN) + dot(dlow, fq, NN))[0:1, :]

    loop(0, heads // 2, 2, attend)
    a_near, a_far, a_diag = [], [], []
    for j in range(QUARTERS):
        a_far.append(links.copy(r["at"].at[1 - b3, core, j], r["ar"].at[1, j], 8))
        a_diag.append(links.copy(r["at"].at[1 - b3, 1 - core, j], r["ar"].at[2, j], 9))
    loop(heads // 2, heads, 2, attend)
    for j in range(QUARTERS):
        a_near.append(links.copy(r["at"].at[b3, 1 - core, j], r["ar"].at[0, j], 1))
    zgrad.start()
    relay(1)
    r["ogb"][pl.ds(0, tokens), :] = r["og"][...]
    for c in og_c:
        c.wait_recv()
    for j in range(2):
        og_d[j].wait_recv()
    for j in range(3):
        r["ogb"][pl.ds((j + 1) * tokens, tokens), :] = r["ogr"][j].astype(BF)
    grad.settle()
    zgrad.climb()

    part, r1, r2, r3 = r["part"], r["r1"], r["r2"], r["r3"]
    half = out_width // 2
    side = (pl.ds(0, half), pl.ds(half, half))
    s1, s2, s3 = {}, {}, {}

    def multiply(j):
        for c in (a_near[j], a_far[j], a_diag[j]):
            c.wait_recv()
        rows = 8 * piece
        r["lhs"][:, pl.ds(0, tokens)] = r["at"][b3, core, j].reshape(rows, tokens).astype(BF)
        for s in range(3):
            r["lhs"][:, pl.ds((s + 1) * tokens, tokens)] = r["ar"][s, j].reshape(rows, tokens).astype(BF)
        tile = 256
        for a in range(2):
            def one(t):
                at = pl.ds(pl.multiple_of(a * half + t * tile, tile), tile)
                out = dot(r["lhs"][...], r["ogb"][:, at], NN)
                part[j, :, :, :, at] = out.reshape(2, 2, 2 * piece, tile)

            loop(0, half // tile, 1, one)
            if a == 0:
                s1[j, a] = links.copy(part.at[j, 1 - b1, :, :, side[a]], r1.at[j, :, :, side[a]], 2)
            else:
                s1[j, a] = links.copy(part.at[j, :, 1 - b2, :, side[a]], r1.at[j, :, :, side[a]], 4)

    def second(j, a):
        s1[j, a].wait_recv()
        for x in range(2):
            if a == 0:
                part[j, b1, x, :, side[a]] += r1[j, x, :, side[a]]
            else:
                part[j, x, b2, :, side[a]] += r1[j, x, :, side[a]]
        if a == 0:
            s2[j, a] = links.copy(part.at[j, b1, 1 - b2, :, side[a]], r2.at[j, :, side[a]], 4)
        else:
            s2[j, a] = links.copy(part.at[j, 1 - b1, b2, :, side[a]], r2.at[j, :, side[a]], 2)

    def third(j, a):
        s2[j, a].wait_recv()
        part[j, b1, b2, :, side[a]] += r2[j, :, side[a]]
        give = pl.ds(pl.multiple_of((1 - b4) * piece, 8), piece)
        s3[j, a] = links.copy(part.at[j, b1, b2, give, side[a]], r3.at[j, :, side[a]], 16)

    def last(j, a):
        s3[j, a].wait_recv()
        keep = pl.ds(pl.multiple_of(b4 * piece, 8), piece)
        wg_ref[pl.ds(j * piece, piece), side[a]] = part[j, b1, b2, keep, side[a]] + r3[j, :, side[a]]

    def local_grads(h):
        at = columns(h)
        fq32, fk32 = features(r["q"][:, at]), features(r["k"][:, at])
        v = r["v"][:, at]
        dn = r["da"][at, :]
        dden = r["dd"][pl.ds(h, 1), :]
        mask = causal()
        scores = jnp.where(mask, dot(r["fk"][:, at], r["fq"][:, at], NT), 0.0)
        dp = jnp.where(mask, mm(v, dn, NN) + dden, 0.0)
        z = jnp.broadcast_to(r["vae"][pl.ds(h, 1), :], (8, HEAD))
        first = lax.broadcasted_iota(jnp.int32, (8, tokens), 0) == 0
        left = jnp.concatenate([dn, jnp.where(first, dden, 0.0)], axis=0)
        right = jnp.concatenate([state.entry(at), z], axis=0)
        dfq = mm(dp, fk32, TN) + mm(left, right, TN)
        dq_ref[:, at] = (dfq * jnp.minimum(fq32, 1.0)).astype(BF)
        g = grad.entry(at)
        dfk = mm(dp, fq32, NN) + mm(v, g, NN) + r["vbe"][pl.ds(h, 1), :]
        dk_ref[:, at] = (dfk * jnp.minimum(fk32, 1.0)).astype(BF)
        dv_ref[:, at] = (mm(scores, dn, NT) + mm(fk32, g, NT)).astype(BF)

    multiply(0)
    grad.join()
    zgrad.finish()
    multiply(1)
    second(0, 0), second(0, 1)
    grad.finish()
    multiply(2)
    third(0, 0), third(0, 1), second(1, 0), second(1, 1)
    loop(0, heads // 4, 2, local_grads)
    multiply(3)
    third(1, 0), third(1, 1), second(2, 0), second(2, 1)
    last(0, 0), last(0, 1)
    loop(heads // 4, heads // 2, 2, local_grads)
    third(2, 0), third(2, 1), second(3, 0), second(3, 1)
    last(1, 0), last(1, 1)
    loop(heads // 2, 3 * heads // 4, 2, local_grads)
    third(3, 0), third(3, 1)
    loop(3 * heads // 4, heads, 2, local_grads)
    last(2, 0), last(2, 1), last(3, 0), last(3, 1)
    links.drain()


def body(queries, keys, values, out_weight, out_grad):
    assert lax.axis_size("seq") == 32
    tokens, width = queries.shape
    out_width = out_grad.shape[1]
    vm = scratch_of(tokens, width, out_width)
    like = jax.ShapeDtypeStruct
    anywhere = pl.BlockSpec(memory_space=pl.ANY)
    inside = pl.BlockSpec(memory_space=pltpu.VMEM)
    dma = pltpu.SemaphoreType.DMA
    return pl.pallas_call(
        functools.partial(kernel, list(vm)),
        out_shape=[like(queries.shape, BF)] * 3 + [like((width // 32, out_width), F32)],
        in_specs=[anywhere] * 5,
        out_specs=[inside] * 4,
        scratch_shapes=[pltpu.VMEM(shape, kind) for shape, kind in vm.values()]
        + [dma((4,)), dma((W_SLOTS,)), dma((COPIES,)), dma((COPIES,))],
        compiler_params=pltpu.CompilerParams(collective_id=0, has_side_effects=True, vmem_limit_bytes=60 << 20),
        cost_estimate=pl.CostEstimate(flops=10_000_000_000, bytes_accessed=16_000_000, transcendentals=0),
    )(queries, keys, values, out_weight, out_grad)


def solution(mesh):
    rows = P(("groups", "seq"), None)
    return jax.shard_map(
        lambda *args: tuple(body(*args)), mesh=mesh, in_specs=(rows, rows, rows, P(), rows),
        out_specs=(rows, rows, rows, rows), check_vma=False)
```

```python
import functools

import jax
import jax.numpy as jnp
from jax import lax
from jax.experimental import pallas as pl
from jax.experimental.pallas import tpu as pltpu
from jax.sharding import PartitionSpec as P

HEAD = 128
MESH = pl.DeviceIdType.MESH
BF = jnp.bfloat16
F32 = jnp.float32
NN = (((1,), (0,)), ((), ()))
NT = (((1,), (1,)), ((), ()))
TN = (((0,), (0,)), ((), ()))
QUARTERS = 4
W_SLOTS = 4
W_ROWS = 256


def dot(a, b, dims):
    return lax.dot_general(a, b, dims, preferred_element_type=F32)


def two(x):
    high = x.astype(BF)
    return high, (x - high.astype(F32)).astype(BF)


def mm(a, b, dims):
    a = (a,) if a.dtype == BF else two(a)
    b = (b,) if b.dtype == BF else two(b)
    total = dot(a[0], b[0], dims)
    if len(a) > 1:
        total += dot(a[1], b[0], dims)
    if len(b) > 1:
        total += dot(a[0], b[1], dims)
    return total


def features(x):
    x = x.astype(F32)
    return jnp.where(x > 0, x + 1.0, jnp.exp(jnp.minimum(x, 0.0)))


def bit_of(x, k):
    return (x // (1 << k)) % 2


def flip(x, mask):
    for k in range(mask.bit_length()):
        if (mask >> k) & 1:
            x = x + (1 - 2 * bit_of(x, k)) * (1 << k)
    return x


def loop(start, stop, unroll, one):
    assert (stop - start) % unroll == 0

    def body(i, carry):
        for j in range(unroll):
            one(start + i * unroll + j)
        return carry

    lax.fori_loop(0, (stop - start) // unroll, body, 0)


def scratch_of(tokens, width, out_width):
    heads, shard = width // HEAD, width // 8
    piece = width // 32 // QUARTERS
    vm = {}
    for name in ("q", "k", "v", "fq", "fk"):
        vm[name] = ((tokens, width), BF)
    vm["og"] = ((tokens, out_width), BF)
    vm["wb"] = ((W_SLOTS, W_ROWS, out_width), BF)
    vm["vt"] = ((width, tokens), BF)
    vm["da"] = ((width, tokens), F32)
    vm["nl"] = ((width, tokens), F32)
    vm["inv"] = ((heads, tokens), F32)
    vm["dd"] = ((heads, tokens), F32)
    for s in ("s", "g"):
        vm[s + "x"] = ((width, HEAD), F32)
        vm[s + "xp"] = ((width, HEAD), F32)
        vm[s + "t"] = ((width // 2, HEAD), F32)
        vm[s + "p"] = ((shard, HEAD), F32)
        for name in ("u", "z", "n"):
            vm[s + name] = ((4, shard, HEAD), F32)
        vm[s + "e"] = ((width, HEAD), F32)
    for s in ("a", "b"):
        vm["v" + s + "b"] = ((8, heads, HEAD), F32)
        vm["v" + s + "p"] = ((heads, HEAD), F32)
        vm["v" + s + "l"] = ((4, heads, HEAD), F32)
        vm["v" + s + "e"] = ((heads, HEAD), F32)
    vm["og32"] = ((tokens, out_width), F32)
    vm["ogr"] = ((3, tokens, out_width), F32)
    vm["ogb"] = ((4 * tokens, out_width), BF)
    vm["at"] = ((2, 2, QUARTERS, 8, piece, tokens), F32)
    vm["ar"] = ((3, QUARTERS, 8, piece, tokens), F32)
    vm["lhs"] = ((QUARTERS, 8 * piece, 4 * tokens), BF)
    vm["dvl"] = ((tokens, width), F32)
    for name in ("dq", "dk", "dv"):
        vm[name] = ((tokens, width), BF)
    vm["wg"] = ((QUARTERS * piece, out_width), F32)
    vm["part"] = ((QUARTERS, 2, 2, 2 * piece, out_width), F32)
    vm["r1"] = ((QUARTERS, 2, 2 * piece, out_width), F32)
    vm["r2"] = ((QUARTERS, 2 * piece, out_width), F32)
    vm["r3"] = ((QUARTERS, piece, out_width), F32)
    return vm


COPIES = 128
OG_CHUNKS = 8


class Links:
    def __init__(self, me, send, recv):
        self.me, self.send, self.recv, self.used, self.sent = me, send, recv, 0, []

    def copy(self, src, dst, mask, when=None):
        i = self.used
        self.used += 1
        made = pltpu.make_async_remote_copy(
            src_ref=src, dst_ref=dst, send_sem=self.send.at[i], recv_sem=self.recv.at[i],
            device_id={"seq": flip(self.me, mask)}, device_id_type=MESH)
        if when is None:
            made.start()
        else:
            pl.when(when)(made.start)
        self.sent.append((made, when))
        return made

    def drain(self):
        for made, when in self.sent:
            if when is None:
                made.wait_send()
            else:
                pl.when(when)(made.wait_send)


class StateScan:
    def __init__(self, links, r, s, later):
        self.links, self.later = links, later
        self.x, self.xp, self.t, self.p = r[s + "x"], r[s + "xp"], r[s + "t"], r[s + "p"]
        self.u, self.z, self.n, self.e = r[s + "u"], r[s + "z"], r[s + "n"], r[s + "e"]
        me = links.me
        self.core, self.chip, self.layer = me % 2, (me // 2) % 4, me // 8
        self.half = self.x.shape[0] // 2
        self.shard = self.p.shape[0]

    def before(self, a, b):
        return a > b if self.later else a < b

    def rows(self, ref, start, size):
        return ref.at[pl.ds(pl.multiple_of(start, 8), size)]

    def give(self):
        at = (1 - self.core) * self.half
        self.c1 = self.links.copy(self.rows(self.x, at, self.half), self.rows(self.xp, at, self.half), 1)

    def give_rest(self):
        at = self.core * self.half
        self.c2 = self.links.copy(self.rows(self.x, at, self.half), self.rows(self.xp, at, self.half), 1)

    def spread(self):
        self.c1.wait_recv()
        at = pl.ds(pl.multiple_of(self.core * self.half, 8), self.half)
        self.t[...] = self.x[at, :] + self.xp[at, :]
        self.c3 = [
            self.links.copy(self.rows(self.t, flip(self.chip, j) * self.shard, self.shard), self.u.at[j], 2 * j)
            for j in (1, 2, 3)]

    def climb(self):
        self.u[0] = self.t[pl.ds(pl.multiple_of(self.chip * self.shard, 8), self.shard), :]
        for c in self.c3:
            c.wait_recv()
        self.p[...] = (self.u[0] + self.u[1]) + (self.u[2] + self.u[3])
        self.c4 = []
        for j in (1, 2, 3):
            other = flip(self.layer, j)
            self.c4.append((j, other, self.links.copy(self.p, self.z.at[j], 8 * j, self.before(self.layer, other))))

    def settle(self):
        self.n[0] = jnp.zeros(self.p.shape, F32)
        for j, other, c in self.c4:
            @pl.when(self.before(other, self.layer))
            def _():
                c.wait_recv()
                self.n[0] = self.n[0] + self.z[j]
        entry = self.n[0]
        mine = pl.multiple_of(self.core * self.half + self.chip * self.shard, 8)
        self.c5 = []
        for i in (3, 2, 1, 0):
            chip = flip(self.chip, i)
            value = entry
            for j in range(4):
                if j != i:
                    value = value + jnp.where(self.before(flip(self.chip, j), chip), self.u[j], 0.0)
            if i:
                self.n[i] = value
                self.c5.append(self.links.copy(self.n.at[i], self.rows(self.e, mine, self.shard), 2 * i))
            else:
                self.e[pl.ds(mine, self.shard), :] = value

    def join(self):
        for c in self.c5:
            c.wait_recv()
        block = self.rows(self.e, self.core * self.half, self.half)
        self.c6 = self.links.copy(block, block, 1)

    def finish(self):
        self.c6.wait_recv()
        self.c2.wait_recv()

    def entry(self, at):
        return self.e[at, :] + jnp.where(self.before(1 - self.core, self.core), self.xp[at, :], 0.0)


class RowScan:
    def __init__(self, links, r, s, later):
        self.links, self.later = links, later
        self.b, self.p, self.l, self.e = r["v" + s + "b"], r["v" + s + "p"], r["v" + s + "l"], r["v" + s + "e"]

    def before(self, a, b):
        return a > b if self.later else a < b

    def start(self):
        self.c1 = [self.links.copy(self.b.at[0], self.b.at[j], j) for j in range(1, 8)]

    def climb(self):
        for c in self.c1:
            c.wait_recv()
        total = self.b[0]
        for j in range(1, 8):
            total = total + self.b[j]
        self.p[...] = total
        self.c2 = [self.links.copy(self.p, self.l.at[j], 8 * j) for j in (1, 2, 3)]

    def finish(self):
        me = self.links.me
        spot, layer = me % 8, me // 8
        total = jnp.zeros(self.e.shape, F32)
        for j in range(1, 8):
            total = total + jnp.where(self.before(flip(spot, j), spot), self.b[j], 0.0)
        for j in (1, 2, 3):
            self.c2[j - 1].wait_recv()
            total = total + jnp.where(self.before(flip(layer, j), layer), self.l[j], 0.0)
        self.e[...] = total


PEERS = (1, 2, 3, 4, 5, 6, 7, 8, 9, 16, 24)


def kernel(names, q_hbm, k_hbm, v_hbm, w_hbm, og_hbm, dq_hbm, dk_hbm, dv_hbm, wg_hbm, *refs):
    r = dict(zip(names, refs))
    load_sem, w_sem, send, recv, store_sem = refs[len(names):]
    dq_ref, dk_ref, dv_ref, wg_ref = r["dq"], r["dk"], r["dv"], r["wg"]
    stores = []

    def store(src, dst):
        made = pltpu.make_async_copy(src, dst, store_sem.at[len(stores)])
        made.start()
        stores.append(made)
    me = lax.axis_index("seq")
    core, b1, b2, b3, b4 = [bit_of(me, k) for k in range(5)]
    tokens, width = r["q"].shape
    out_width = r["og"].shape[1]
    heads = width // HEAD
    piece = r["r3"].shape[1]
    links = Links(me, send, recv)

    loads = {}
    for i, (name, src) in enumerate((("k", k_hbm), ("v", v_hbm), ("og", og_hbm), ("q", q_hbm))):
        loads[name] = pltpu.make_async_copy(src, r[name], load_sem.at[i])
        loads[name].start()

    def w_load(i):
        return pltpu.make_async_copy(
            w_hbm.at[pl.ds(pl.multiple_of(i * W_ROWS, W_ROWS), W_ROWS)], r["wb"].at[i % W_SLOTS], w_sem.at[i % W_SLOTS])

    for i in range(W_SLOTS):
        w_load(i).start()

    barrier = pltpu.get_barrier_semaphore()
    for mask in PEERS:
        pl.semaphore_signal(barrier, inc=1, device_id={"seq": flip(me, mask)}, device_id_type=MESH)

    state = StateScan(links, r, "s", False)
    grad = StateScan(links, r, "g", True)
    zsum = RowScan(links, r, "a", False)
    zgrad = RowScan(links, r, "b", True)

    def columns(h):
        return pl.ds(pl.multiple_of(h * HEAD, HEAD), HEAD)

    def theirs_first(i):
        return (i + (1 - core) * (heads // 2)) % heads

    def causal():
        shape = (tokens, tokens)
        return lax.broadcasted_iota(jnp.int32, shape, 0) <= lax.broadcasted_iota(jnp.int32, shape, 1)

    def sums(i):
        h = theirs_first(i)
        at = columns(h)
        fk = features(r["k"][:, at])
        r["va" + "b"][0, pl.ds(h, 1), :] = jnp.sum(fk, axis=0, keepdims=True)
        r["fk"][:, at] = fk.astype(BF)
        vt = r["v"][:, at].T
        r["vt"][at, :] = vt
        r["sx"][at, :] = mm(vt, fk, NN)

    step = out_width // OG_CHUNKS
    og_z, og_c, og_d = {}, {}, {}

    def offer(*chunks):
        for j in chunks:
            at = pl.ds(j * step, step)
            og_z[j] = links.copy(r["og32"].at[:, at], r["ogr"].at[1, :, at], 8)

    def share(*chunks):
        for j in chunks:
            at = pl.ds(j * step, step)
            og_c[j] = links.copy(r["og32"].at[:, at], r["ogr"].at[0, :, at], 1)

    def relay(*chunks):
        for j in chunks:
            at = pl.ds(j * step, step)
            og_z[j].wait_recv()
            og_d[j] = links.copy(r["ogr"].at[1, :, at], r["ogr"].at[2, :, at], 1)

    def take(*chunks):
        for j in chunks:
            at = pl.ds(j * step, step)
            og_c[j].wait_recv()
            og_d[j].wait_recv()
            r["ogb"][pl.ds(0, tokens), at] = r["og"][:, at]
            for i in range(3):
                r["ogb"][pl.ds((i + 1) * tokens, tokens), at] = r["ogr"][i, :, at].astype(BF)

    loads["k"].wait()
    loads["v"].wait()
    loop(0, heads // 2, 2, sums)
    pl.semaphore_wait(barrier, len(PEERS))
    state.give()
    loads["og"].wait()
    r["og32"][...] = r["og"][...].astype(F32)
    offer(0, 1, 2)
    loop(heads // 2, heads, 2, sums)
    state.spread()
    zsum.start()
    state.give_rest()

    def project(i):
        w_load(i).wait()
        rows = pl.ds(pl.multiple_of(i * W_ROWS, W_ROWS), W_ROWS)
        r["da"][rows, :] = dot(r["wb"][i % W_SLOTS], r["og"][...], NT)

        @pl.when(i + W_SLOTS < width // W_ROWS)
        def _():
            w_load(i + W_SLOTS).start()

    loop(0, width // W_ROWS, 1, project)
    zsum.climb()
    loads["q"].wait()

    def query_features(h):
        r["fq"][:, columns(h)] = features(r["q"][:, columns(h)]).astype(BF)

    loop(0, heads, 2, query_features)
    state.climb()
    zsum.finish()

    def rows_of(x, count):
        return [jnp.broadcast_to(y, (count, y.shape[1])) for y in two(x)]

    def local(i):
        h = theirs_first(i)
        at = columns(h)
        fq, fk = r["fq"][:, at], r["fk"][:, at]
        scores = jnp.where(causal(), dot(fk, fq, NT), 0.0)
        z = r["vae"][pl.ds(h, 1), :]
        zhigh, zlow = rows_of(z, 16)
        den = jnp.sum(scores, axis=0, keepdims=True) + (dot(zhigh, fq, NT) + dot(zlow, fq, NT))[0:1, :]
        inv = 1.0 / den
        r["inv"][pl.ds(h, 1), :] = inv
        r["nl"][at, :] = mm(r["vt"][at, :], scores, NN)
        dn = r["da"][at, :] * inv
        r["da"][at, :] = dn
        r["gx"][at, :] = mm(dn, features(r["q"][:, at]), NN)

    loop(0, heads // 2, 2, local)
    grad.give()
    share(0, 1, 2)
    loop(heads // 2, heads, 2, local)
    grad.give_rest()
    offer(3)
    grad.spread()
    relay(0, 1, 2)
    state.settle()
    grad.climb()
    offer(4)
    share(3, 4)
    state.join()
    offer(5)
    share(5)
    state.finish()

    group = heads // 4

    def attend(i):
        far = i // (heads // 2)
        within = i % (heads // 2)
        low = b3 * far + (1 - b3) * (1 - far)
        h = (within // group) * (2 * group) + low * group + within % group
        at = columns(h)
        fq = r["fq"][:, at]
        high, rest = two(state.entry(at))
        att = (r["nl"][at, :] + dot(high, fq, NT) + dot(rest, fq, NT)) * r["inv"][pl.ds(h, 1), :]
        slot = bit_of(h, 0) * 4 + bit_of(h, 1) * 2 + bit_of(h, 3)
        for c in range(2):
            for j in range(QUARTERS):
                start = (c * QUARTERS + j) * piece
                r["at"][low, c, j, slot] = att[start:start + piece, :]
        dden = -jnp.sum(r["da"][at, :] * att, axis=0, keepdims=True)
        r["dd"][pl.ds(h, 1), :] = dden
        dhigh, dlow = rows_of(dden, 16)
        r["vbb"][0, pl.ds(h, 1), :] = (dot(dhigh, fq, NN) + dot(dlow, fq, NN))[0:1, :]

    loop(0, heads // 2, 2, attend)
    a_near, a_far, a_diag = {}, {}, {}

    def pass_on(j):
        a_far[j] = links.copy(r["at"].at[1 - b3, core, j], r["ar"].at[1, j], 8)
        a_diag[j] = links.copy(r["at"].at[1 - b3, 1 - core, j], r["ar"].at[2, j], 9)

    pass_on(0)
    loop(heads // 2, heads, 2, attend)
    for j in range(QUARTERS):
        a_near[j] = links.copy(r["at"].at[b3, 1 - core, j], r["ar"].at[0, j], 1)
    zgrad.start()
    relay(3)
    take(0, 1, 2)
    pass_on(1)

    part, r1, r2, r3 = r["part"], r["r1"], r["r2"], r["r3"]
    tile = 256

    def gather(j):
        for c in (a_near[j], a_far[j], a_diag[j]):
            c.wait_recv()
        rows = 8 * piece
        r["lhs"][j, :, pl.ds(0, tokens)] = r["at"][b3, core, j].reshape(rows, tokens).astype(BF)
        for i in range(3):
            r["lhs"][j, :, pl.ds((i + 1) * tokens, tokens)] = r["ar"][i, j].reshape(rows, tokens).astype(BF)

    half, quarter = out_width // 2, out_width // 4
    units = [((j, 1), (0, half)) for j in range(QUARTERS)]
    for at in (half, half + quarter):
        units += [((j, 2), (at, quarter)) for j in range(0, QUARTERS, 2)]
    s1, s2, s3 = {}, {}, {}

    def place(u, a):
        (j, count), (at, size) = units[u]
        return pl.ds(j, count), pl.ds(at + a * (size // 2), size // 2)

    def multiply(u):
        (j, count), (at, size) = units[u]

        def one(t):
            cols = pl.ds(pl.multiple_of(at + t * tile, tile), tile)
            left = r["lhs"][pl.ds(j, count)].reshape(count * 8 * piece, 4 * tokens)
            out = dot(left, r["ogb"][:, cols], NN)
            part[pl.ds(j, count), :, :, :, cols] = out.reshape(count, 2, 2, 2 * piece, tile)

        loop(0, size // tile, 1, one)

    def first(u):
        rows, cols = place(u, 0)
        s1[u, 0] = links.copy(part.at[rows, 1 - b1, :, :, cols], r1.at[rows, :, :, cols], 2)
        rows, cols = place(u, 1)
        s1[u, 1] = links.copy(part.at[rows, :, 1 - b2, :, cols], r1.at[rows, :, :, cols], 4)

    def second(u):
        for a in range(2):
            rows, cols = place(u, a)
            s1[u, a].wait_recv()
            for x in range(2):
                if a == 0:
                    part[rows, b1, x, :, cols] += r1[rows, x, :, cols]
                else:
                    part[rows, x, b2, :, cols] += r1[rows, x, :, cols]
            if a == 0:
                s2[u, a] = links.copy(part.at[rows, b1, 1 - b2, :, cols], r2.at[rows, :, cols], 4)
            else:
                s2[u, a] = links.copy(part.at[rows, 1 - b1, b2, :, cols], r2.at[rows, :, cols], 2)

    def third(u):
        for a in range(2):
            rows, cols = place(u, a)
            s2[u, a].wait_recv()
            part[rows, b1, b2, :, cols] += r2[rows, :, cols]
            give = pl.ds(pl.multiple_of((1 - b4) * piece, 8), piece)
            s3[u, a] = links.copy(part.at[rows, b1, b2, give, cols], r3.at[rows, :, cols], 16)

    def last(u):
        keep = pl.ds(pl.multiple_of(b4 * piece, 8), piece)
        for a in range(2):
            rows, cols = place(u, a)
            (j, count), (_, size) = units[u]
            s3[u, a].wait_recv()
            total = part[rows, b1, b2, keep, cols] + r3[rows, :, cols]
            at = pl.ds(j * piece, count * piece)
            wg_ref[at, cols] = total.reshape(count * piece, size // 2)
            store(wg_ref.at[at, cols], wg_hbm.at[at, cols])

    def local_grads(h):
        at = columns(h)
        fq32, fk32 = features(r["q"][:, at]), features(r["k"][:, at])
        v = r["v"][:, at]
        dn = r["da"][at, :]
        dden = r["dd"][pl.ds(h, 1), :]
        mask = causal()
        scores = jnp.where(mask, dot(r["fk"][:, at], r["fq"][:, at], NT), 0.0)
        dp = jnp.where(mask, mm(v, dn, NN) + dden, 0.0)
        z = jnp.broadcast_to(r["vae"][pl.ds(h, 1), :], (8, HEAD))
        top = lax.broadcasted_iota(jnp.int32, (8, tokens), 0) == 0
        left = jnp.concatenate([dn, jnp.where(top, dden, 0.0)], axis=0)
        right = jnp.concatenate([state.entry(at), z], axis=0)
        dfq = mm(dp, fk32, TN) + mm(left, right, TN)
        dq_ref[:, at] = (dfq * jnp.minimum(fq32, 1.0)).astype(BF)
        dfk = mm(dp, fq32, NN)
        for i in range(tokens // HEAD):
            r["nl"][at, pl.ds(i * HEAD, HEAD)] = dfk[i * HEAD:(i + 1) * HEAD, :]
        r["dvl"][:, at] = mm(scores, dn, NT)

    def later_grads(h):
        at = columns(h)
        fk32 = features(r["k"][:, at])
        g = grad.entry(at)
        dfk = jnp.concatenate([r["nl"][at, pl.ds(i * HEAD, HEAD)] for i in range(tokens // HEAD)], axis=0)
        dfk = dfk + mm(r["v"][:, at], g, NN) + r["vbe"][pl.ds(h, 1), :]
        dk_ref[:, at] = (dfk * jnp.minimum(fk32, 1.0)).astype(BF)
        dv_ref[:, at] = (r["dvl"][:, at] + mm(fk32, g, NT)).astype(BF)

    def early(start, stop):
        loop(start, stop, 2, local_grads)
        at = pl.ds(start * HEAD, (stop - start) * HEAD)
        store(dq_ref.at[:, at], dq_hbm.at[:, at])

    def late(start, stop):
        loop(start, stop, 2, later_grads)
        at = pl.ds(start * HEAD, (stop - start) * HEAD)
        store(dk_ref.at[:, at], dk_hbm.at[:, at])
        store(dv_ref.at[:, at], dv_hbm.at[:, at])

    early(0, 2)
    take(3)
    gather(0)
    pass_on(2)
    multiply(0)
    first(0)
    grad.settle()
    zgrad.climb()
    relay(4)
    early(2, 4)
    gather(1)
    pass_on(3)
    multiply(1)
    first(1)
    grad.join()
    zgrad.finish()
    relay(5)
    gather(2)
    offer(6)
    share(6)
    multiply(2)
    second(0)
    first(2)
    early(4, 6)
    gather(3)
    offer(7)
    share(7)
    multiply(3)
    second(1)
    third(0)
    first(3)
    grad.finish()
    early(6, 8)
    take(4, 5)
    multiply(4)
    second(2)
    third(1)
    first(4)
    last(0)
    early(8, 10)
    relay(6)
    multiply(5)
    second(3)
    third(2)
    first(5)
    last(1)
    early(10, 12)
    relay(7)
    take(6, 7)
    multiply(6)
    second(4)
    third(3)
    first(6)
    last(2)
    early(12, 14)
    multiply(7)
    second(5)
    third(4)
    first(7)
    last(3)
    early(14, 16)
    late(0, 4)
    second(6)
    third(5)
    last(4)
    late(4, 8)
    second(7)
    third(6)
    last(5)
    late(8, 12)
    third(7)
    last(6)
    late(12, 16)
    last(7)
    for made in stores:
        made.wait()
    links.drain()


def hand_over(count, *refs):
    ins, outs, held, sem = refs[:count], refs[count:2 * count], refs[2 * count:3 * count], refs[3 * count]
    moves = []
    for i in range(count):
        rows = ins[i].shape[0] // 2
        for j in range(2):
            at = pl.ds(j * rows, rows)
            n = len(moves)
            moves.append((pltpu.make_async_copy(ins[i].at[at], held[i].at[at], sem.at[2 * n]),
                          pltpu.make_async_copy(held[i].at[at], outs[i].at[at], sem.at[2 * n + 1])))
    for first, _ in moves:
        first.start()
    for first, second in moves:
        first.wait()
        second.start()
    for _, second in moves:
        second.wait()


def body(queries, keys, values, out_weight, out_grad):
    assert lax.axis_size("seq") == 32
    tokens, width = queries.shape
    out_width = out_grad.shape[1]
    vm = scratch_of(tokens, width, out_width)
    like = jax.ShapeDtypeStruct
    anywhere = pl.BlockSpec(memory_space=pl.ANY)
    dma = pltpu.SemaphoreType.DMA
    made = pl.pallas_call(
        functools.partial(kernel, list(vm)),
        out_shape=[like(queries.shape, BF)] * 3 + [like((width // 32, out_width), F32)],
        in_specs=[anywhere] * 5,
        out_specs=[pl.BlockSpec(memory_space=pltpu.HBM)] * 4,
        scratch_shapes=[pltpu.VMEM(shape, kind) for shape, kind in vm.values()]
        + [dma((4,)), dma((W_SLOTS,)), dma((COPIES,)), dma((COPIES,)), dma((48,))],
        compiler_params=pltpu.CompilerParams(collective_id=0, has_side_effects=True, vmem_limit_bytes=58 << 20),
        cost_estimate=pl.CostEstimate(flops=10_000_000_000, bytes_accessed=16_000_000, transcendentals=0),
    )(queries, keys, values, out_weight, out_grad)
    return pl.pallas_call(
        functools.partial(hand_over, len(made)),
        out_shape=[like(x.shape, x.dtype) for x in made],
        in_specs=[pl.BlockSpec(memory_space=pltpu.HBM)] * len(made),
        out_specs=[pl.BlockSpec(memory_space=pltpu.HBM)] * len(made),
        scratch_shapes=[pltpu.VMEM(x.shape, x.dtype) for x in made] + [dma((4 * len(made),))],
        compiler_params=pltpu.CompilerParams(vmem_limit_bytes=60 << 20),
    )(*made)


def solution(mesh):
    rows = P(("groups", "seq"), None)
    return jax.shard_map(
        lambda *args: tuple(body(*args)), mesh=mesh, in_specs=(rows, rows, rows, P(), rows),
        out_specs=(rows, rows, rows, rows), check_vma=False)
```

```python
import functools

import jax
import jax.numpy as jnp
from jax import lax
from jax.experimental import pallas as pl
from jax.experimental.pallas import tpu as pltpu
from jax.sharding import PartitionSpec as P

HEAD = 128
MESH = pl.DeviceIdType.MESH
BF = jnp.bfloat16
F32 = jnp.float32
NN = (((1,), (0,)), ((), ()))
NT = (((1,), (1,)), ((), ()))
TN = (((0,), (0,)), ((), ()))
QUARTERS = 4
W_SLOTS = 4
PIECES = 4
W_ROWS = 256


def dot(a, b, dims):
    return lax.dot_general(a, b, dims, preferred_element_type=F32)


def two(x):
    high = x.astype(BF)
    return high, (x - high.astype(F32)).astype(BF)


def mm(a, b, dims):
    a = (a,) if a.dtype == BF else two(a)
    b = (b,) if b.dtype == BF else two(b)
    total = dot(a[0], b[0], dims)
    if len(a) > 1:
        total += dot(a[1], b[0], dims)
    if len(b) > 1:
        total += dot(a[0], b[1], dims)
    return total


def features(x):
    x = x.astype(F32)
    return jnp.where(x > 0, x + 1.0, jnp.exp(jnp.minimum(x, 0.0)))


def bit_of(x, k):
    return (x // (1 << k)) % 2


def flip(x, mask):
    for k in range(mask.bit_length()):
        if (mask >> k) & 1:
            x = x + (1 - 2 * bit_of(x, k)) * (1 << k)
    return x


def loop(start, stop, unroll, one):
    assert (stop - start) % unroll == 0

    def body(i, carry):
        for j in range(unroll):
            one(start + i * unroll + j)
        return carry

    lax.fori_loop(0, (stop - start) // unroll, body, 0)


def scratch_of(tokens, width, out_width):
    heads, shard = width // HEAD, width // 8
    piece = width // 32 // QUARTERS
    vm = {}
    for name in ("q", "k", "v", "fq", "fk"):
        vm[name] = ((tokens, width), BF)
    vm["og"] = ((tokens, out_width), BF)
    vm["wb"] = ((W_SLOTS, W_ROWS, out_width), BF)
    vm["vt"] = ((width, tokens), BF)
    vm["da"] = ((width, tokens), F32)
    vm["nl"] = ((width, tokens), F32)
    vm["inv"] = ((heads, tokens), F32)
    vm["dd"] = ((heads, tokens), F32)
    for s in ("s", "g"):
        vm[s + "x"] = ((width, HEAD), F32)
        vm[s + "xp"] = ((width, HEAD), F32)
        vm[s + "t"] = ((width // 2, HEAD), F32)
        vm[s + "p"] = ((shard, HEAD), F32)
        for name in ("u", "z", "n"):
            vm[s + name] = ((4, shard, HEAD), F32)
        vm[s + "e"] = ((width, HEAD), F32)
    for s in ("a", "b"):
        vm["v" + s + "b"] = ((8, heads, HEAD), F32)
        vm["v" + s + "p"] = ((heads, HEAD), F32)
        vm["v" + s + "l"] = ((4, heads, HEAD), F32)
        vm["v" + s + "e"] = ((heads, HEAD), F32)
    vm["og32"] = ((tokens, out_width), F32)
    vm["ogr"] = ((3, tokens, out_width), F32)
    vm["ogb"] = ((4 * tokens, out_width), BF)
    vm["at"] = ((2, 2, QUARTERS, 8, piece, tokens), F32)
    vm["ar"] = ((3, QUARTERS, 8, piece, tokens), F32)
    vm["lhs"] = ((QUARTERS, 8 * piece, 4 * tokens), BF)
    vm["dvl"] = ((tokens, width), F32)
    for name in ("dq", "dk", "dv"):
        vm[name] = ((tokens, width), BF)
    vm["wg"] = ((QUARTERS * piece, out_width), F32)
    vm["part"] = ((QUARTERS, 2, 2, 2 * piece, out_width), F32)
    vm["r1"] = ((QUARTERS, 2, 2 * piece, out_width), F32)
    vm["r2"] = ((QUARTERS, 2 * piece, out_width), F32)
    vm["r3"] = ((QUARTERS, piece, out_width), F32)
    return vm


COPIES = 128
OG_CHUNKS = 8


class Links:
    def __init__(self, me, send, recv):
        self.me, self.send, self.recv, self.used, self.sent = me, send, recv, 0, []

    def copy(self, src, dst, mask, when=None):
        i = self.used
        self.used += 1
        made = pltpu.make_async_remote_copy(
            src_ref=src, dst_ref=dst, send_sem=self.send.at[i], recv_sem=self.recv.at[i],
            device_id={"seq": flip(self.me, mask)}, device_id_type=MESH)
        if when is None:
            made.start()
        else:
            pl.when(when)(made.start)
        self.sent.append((made, when))
        return made

    def drain(self):
        for made, when in self.sent:
            if when is None:
                made.wait_send()
            else:
                pl.when(when)(made.wait_send)


class StateScan:
    def __init__(self, links, r, s, later):
        self.links, self.later = links, later
        self.x, self.xp, self.t, self.p = r[s + "x"], r[s + "xp"], r[s + "t"], r[s + "p"]
        self.u, self.z, self.n, self.e = r[s + "u"], r[s + "z"], r[s + "n"], r[s + "e"]
        me = links.me
        self.core, self.chip, self.layer = me % 2, (me // 2) % 4, me // 8
        self.half = self.x.shape[0] // 2
        self.shard = self.p.shape[0]

    def before(self, a, b):
        return a > b if self.later else a < b

    def rows(self, ref, start, size):
        return ref.at[pl.ds(pl.multiple_of(start, 8), size)]

    def give(self):
        at = (1 - self.core) * self.half
        self.c1 = self.links.copy(self.rows(self.x, at, self.half), self.rows(self.xp, at, self.half), 1)

    def give_rest(self):
        at = self.core * self.half
        self.c2 = self.links.copy(self.rows(self.x, at, self.half), self.rows(self.xp, at, self.half), 1)

    def spread(self):
        self.c1.wait_recv()
        at = pl.ds(pl.multiple_of(self.core * self.half, 8), self.half)
        self.t[...] = self.x[at, :] + self.xp[at, :]
        self.c3 = [
            self.links.copy(self.rows(self.t, flip(self.chip, j) * self.shard, self.shard), self.u.at[j], 2 * j)
            for j in (1, 2, 3)]

    def climb(self):
        self.u[0] = self.t[pl.ds(pl.multiple_of(self.chip * self.shard, 8), self.shard), :]
        for c in self.c3:
            c.wait_recv()
        self.p[...] = (self.u[0] + self.u[1]) + (self.u[2] + self.u[3])
        self.c4 = []
        for j in (1, 2, 3):
            other = flip(self.layer, j)
            self.c4.append((j, other, self.links.copy(self.p, self.z.at[j], 8 * j, self.before(self.layer, other))))

    def settle(self):
        self.n[0] = jnp.zeros(self.p.shape, F32)
        for j, other, c in self.c4:
            @pl.when(self.before(other, self.layer))
            def _():
                c.wait_recv()
                self.n[0] = self.n[0] + self.z[j]
        entry = self.n[0]
        mine = pl.multiple_of(self.core * self.half + self.chip * self.shard, 8)
        self.c5 = []
        for i in (3, 2, 1, 0):
            chip = flip(self.chip, i)
            value = entry
            for j in range(4):
                if j != i:
                    value = value + jnp.where(self.before(flip(self.chip, j), chip), self.u[j], 0.0)
            if i:
                self.n[i] = value
                self.c5.append(self.links.copy(self.n.at[i], self.rows(self.e, mine, self.shard), 2 * i))
            else:
                self.e[pl.ds(mine, self.shard), :] = value

    def join(self):
        for c in self.c5:
            c.wait_recv()
        block = self.rows(self.e, self.core * self.half, self.half)
        self.c6 = self.links.copy(block, block, 1)

    def finish(self):
        self.c6.wait_recv()
        self.c2.wait_recv()

    def entry(self, at):
        return self.e[at, :] + jnp.where(self.before(1 - self.core, self.core), self.xp[at, :], 0.0)


class RowScan:
    def __init__(self, links, r, s, later):
        self.links, self.later = links, later
        self.b, self.p, self.l, self.e = r["v" + s + "b"], r["v" + s + "p"], r["v" + s + "l"], r["v" + s + "e"]

    def before(self, a, b):
        return a > b if self.later else a < b

    def start(self):
        self.c1 = [self.links.copy(self.b.at[0], self.b.at[j], j) for j in range(1, 8)]

    def climb(self):
        for c in self.c1:
            c.wait_recv()
        total = self.b[0]
        for j in range(1, 8):
            total = total + self.b[j]
        self.p[...] = total
        self.c2 = [self.links.copy(self.p, self.l.at[j], 8 * j) for j in (1, 2, 3)]

    def finish(self):
        me = self.links.me
        spot, layer = me % 8, me // 8
        total = jnp.zeros(self.e.shape, F32)
        for j in range(1, 8):
            total = total + jnp.where(self.before(flip(spot, j), spot), self.b[j], 0.0)
        for j in (1, 2, 3):
            self.c2[j - 1].wait_recv()
            total = total + jnp.where(self.before(flip(layer, j), layer), self.l[j], 0.0)
        self.e[...] = total


PEERS = (1, 2, 3, 4, 5, 6, 7, 8, 9, 16, 24)


def kernel(names, q_hbm, k_hbm, v_hbm, w_hbm, og_hbm, dq_hbm, dk_hbm, dv_hbm, wg_hbm, *refs):
    r = dict(zip(names, refs))
    load_sem, w_sem, send, recv, store_sem = refs[len(names):]
    dq_ref, dk_ref, dv_ref, wg_ref = r["dq"], r["dk"], r["dv"], r["wg"]
    stores = []

    def store(src, dst):
        made = pltpu.make_async_copy(src, dst, store_sem.at[len(stores)])
        made.start()
        stores.append(made)
    me = lax.axis_index("seq")
    core, b1, b2, b3, b4 = [bit_of(me, k) for k in range(5)]
    tokens, width = r["q"].shape
    out_width = r["og"].shape[1]
    heads = width // HEAD
    piece = r["r3"].shape[1]
    links = Links(me, send, recv)

    loads = {}
    for i, (name, src) in enumerate((("k", k_hbm), ("v", v_hbm), ("og", og_hbm), ("q", q_hbm))):
        loads[name] = pltpu.make_async_copy(src, r[name], load_sem.at[i])
        loads[name].start()

    def w_load(i):
        return pltpu.make_async_copy(
            w_hbm.at[pl.ds(pl.multiple_of(i * W_ROWS, W_ROWS), W_ROWS)], r["wb"].at[i % W_SLOTS], w_sem.at[i % W_SLOTS])

    for i in range(W_SLOTS):
        w_load(i).start()

    barrier = pltpu.get_barrier_semaphore()
    for mask in PEERS:
        pl.semaphore_signal(barrier, inc=1, device_id={"seq": flip(me, mask)}, device_id_type=MESH)

    state = StateScan(links, r, "s", False)
    grad = StateScan(links, r, "g", True)
    zsum = RowScan(links, r, "a", False)
    zgrad = RowScan(links, r, "b", True)

    def columns(h):
        return pl.ds(pl.multiple_of(h * HEAD, HEAD), HEAD)

    def theirs_first(i):
        return (i + (1 - core) * (heads // 2)) % heads

    def causal():
        shape = (tokens, tokens)
        return lax.broadcasted_iota(jnp.int32, shape, 0) <= lax.broadcasted_iota(jnp.int32, shape, 1)

    def sums(i):
        h = theirs_first(i)
        at = columns(h)
        fk = features(r["k"][:, at])
        r["va" + "b"][0, pl.ds(h, 1), :] = jnp.sum(fk, axis=0, keepdims=True)
        r["fk"][:, at] = fk.astype(BF)
        vt = r["v"][:, at].T
        r["vt"][at, :] = vt
        r["sx"][at, :] = mm(vt, fk, NN)

    step = out_width // OG_CHUNKS
    og_z, og_c, og_d = {}, {}, {}

    def offer(*chunks):
        for j in chunks:
            at = pl.ds(j * step, step)
            og_z[j] = links.copy(r["og32"].at[:, at], r["ogr"].at[1, :, at], 8)

    def share(*chunks):
        for j in chunks:
            at = pl.ds(j * step, step)
            og_c[j] = links.copy(r["og32"].at[:, at], r["ogr"].at[0, :, at], 1)

    def relay(*chunks):
        for j in chunks:
            at = pl.ds(j * step, step)
            og_z[j].wait_recv()
            og_d[j] = links.copy(r["ogr"].at[1, :, at], r["ogr"].at[2, :, at], 1)

    def take(*chunks):
        for j in chunks:
            at = pl.ds(j * step, step)
            og_c[j].wait_recv()
            og_d[j].wait_recv()
            r["ogb"][pl.ds(0, tokens), at] = r["og"][:, at]
            for i in range(3):
                r["ogb"][pl.ds((i + 1) * tokens, tokens), at] = r["ogr"][i, :, at].astype(BF)

    loads["k"].wait()
    loads["v"].wait()
    loop(0, heads // 2, 2, sums)
    pl.semaphore_wait(barrier, len(PEERS))
    state.give()
    loads["og"].wait()
    r["og32"][...] = r["og"][...].astype(F32)
    offer(0, 1, 2)
    loop(heads // 2, heads, 2, sums)
    state.spread()
    zsum.start()
    state.give_rest()

    def project(i):
        w_load(i).wait()
        rows = pl.ds(pl.multiple_of(i * W_ROWS, W_ROWS), W_ROWS)
        r["da"][rows, :] = dot(r["wb"][i % W_SLOTS], r["og"][...], NT)

        @pl.when(i + W_SLOTS < width // W_ROWS)
        def _():
            w_load(i + W_SLOTS).start()

    loop(0, width // W_ROWS, 1, project)
    zsum.climb()
    loads["q"].wait()

    def query_features(h):
        r["fq"][:, columns(h)] = features(r["q"][:, columns(h)]).astype(BF)

    loop(0, heads, 2, query_features)
    state.climb()
    zsum.finish()

    def rows_of(x, count):
        return [jnp.broadcast_to(y, (count, y.shape[1])) for y in two(x)]

    def local(i):
        h = theirs_first(i)
        at = columns(h)
        fq, fk = r["fq"][:, at], r["fk"][:, at]
        scores = jnp.where(causal(), dot(fk, fq, NT), 0.0)
        z = r["vae"][pl.ds(h, 1), :]
        zhigh, zlow = rows_of(z, 16)
        den = jnp.sum(scores, axis=0, keepdims=True) + (dot(zhigh, fq, NT) + dot(zlow, fq, NT))[0:1, :]
        inv = 1.0 / den
        r["inv"][pl.ds(h, 1), :] = inv
        r["nl"][at, :] = mm(r["vt"][at, :], scores, NN)
        dn = r["da"][at, :] * inv
        r["da"][at, :] = dn
        r["gx"][at, :] = mm(dn, features(r["q"][:, at]), NN)

    loop(0, heads // 2, 2, local)
    grad.give()
    share(0, 1, 2)
    offer(3)
    loop(heads // 2, heads, 2, local)
    grad.give_rest()
    grad.spread()
    relay(0, 1, 2)
    state.settle()
    grad.climb()
    offer(4)
    state.join()
    offer(5)
    state.finish()

    group = heads // 4

    def attend(i):
        far = i // (heads // 2)
        within = i % (heads // 2)
        low = b3 * far + (1 - b3) * (1 - far)
        h = (within // group) * (2 * group) + low * group + within % group
        at = columns(h)
        fq = r["fq"][:, at]
        high, rest = two(state.entry(at))
        att = (r["nl"][at, :] + dot(high, fq, NT) + dot(rest, fq, NT)) * r["inv"][pl.ds(h, 1), :]
        slot = bit_of(h, 0) * 4 + bit_of(h, 1) * 2 + bit_of(h, 3)
        for c in range(2):
            for j in range(QUARTERS):
                start = (c * QUARTERS + j) * piece
                r["at"][low, c, j, slot] = att[start:start + piece, :]
        dden = -jnp.sum(r["da"][at, :] * att, axis=0, keepdims=True)
        r["dd"][pl.ds(h, 1), :] = dden
        dhigh, dlow = rows_of(dden, 16)
        r["vbb"][0, pl.ds(h, 1), :] = (dot(dhigh, fq, NN) + dot(dlow, fq, NN))[0:1, :]

    loop(0, heads // 2, 2, attend)
    a_near, a_far, a_diag = {}, {}, {}

    def pass_on(j):
        a_far[j] = links.copy(r["at"].at[1 - b3, core, j], r["ar"].at[1, j], 8)
        a_diag[j] = links.copy(r["at"].at[1 - b3, 1 - core, j], r["ar"].at[2, j], 9)

    pass_on(0)
    loop(heads // 2, heads, 2, attend)
    for j in range(QUARTERS):
        a_near[j] = links.copy(r["at"].at[b3, 1 - core, j], r["ar"].at[0, j], 1)
    zgrad.start()
    share(3, 4, 5)
    relay(3)
    take(0, 1, 2)
    pass_on(1)

    part, r1, r2, r3 = r["part"], r["r1"], r["r2"], r["r3"]
    tile = 256

    def gather(j):
        for c in (a_near[j], a_far[j], a_diag[j]):
            c.wait_recv()
        rows = 8 * piece
        r["lhs"][j, :, pl.ds(0, tokens)] = r["at"][b3, core, j].reshape(rows, tokens).astype(BF)
        for i in range(3):
            r["lhs"][j, :, pl.ds((i + 1) * tokens, tokens)] = r["ar"][i, j].reshape(rows, tokens).astype(BF)

    half, quarter = out_width // 2, out_width // 4
    units = [((j, 1), (0, half)) for j in range(QUARTERS)]
    for at in (half, half + quarter):
        units += [((j, 2), (at, quarter)) for j in range(0, QUARTERS, 2)]
    s1, s2, s3 = {}, {}, {}

    def place(u, a):
        (j, count), (at, size) = units[u]
        return pl.ds(j, count), pl.ds(at + a * (size // 2), size // 2)

    def multiply(u):
        (j, count), (at, size) = units[u]

        def one(t):
            cols = pl.ds(pl.multiple_of(at + t * tile, tile), tile)
            left = r["lhs"][pl.ds(j, count)].reshape(count * 8 * piece, 4 * tokens)
            out = dot(left, r["ogb"][:, cols], NN)
            part[pl.ds(j, count), :, :, :, cols] = out.reshape(count, 2, 2, 2 * piece, tile)

        loop(0, size // tile, 1, one)

    def first(u):
        rows, cols = place(u, 0)
        s1[u, 0] = links.copy(part.at[rows, 1 - b1, :, :, cols], r1.at[rows, :, :, cols], 2)
        rows, cols = place(u, 1)
        s1[u, 1] = links.copy(part.at[rows, :, 1 - b2, :, cols], r1.at[rows, :, :, cols], 4)

    def second(u):
        for a in range(2):
            rows, cols = place(u, a)
            s1[u, a].wait_recv()
            for x in range(2):
                if a == 0:
                    part[rows, b1, x, :, cols] += r1[rows, x, :, cols]
                else:
                    part[rows, x, b2, :, cols] += r1[rows, x, :, cols]
            if a == 0:
                s2[u, a] = links.copy(part.at[rows, b1, 1 - b2, :, cols], r2.at[rows, :, cols], 4)
            else:
                s2[u, a] = links.copy(part.at[rows, 1 - b1, b2, :, cols], r2.at[rows, :, cols], 2)

    def third(u):
        for a in range(2):
            rows, cols = place(u, a)
            s2[u, a].wait_recv()
            part[rows, b1, b2, :, cols] += r2[rows, :, cols]
            give = pl.ds(pl.multiple_of((1 - b4) * piece, 8), piece)
            s3[u, a] = links.copy(part.at[rows, b1, b2, give, cols], r3.at[rows, :, cols], 16)

    def last(u):
        keep = pl.ds(pl.multiple_of(b4 * piece, 8), piece)
        for a in range(2):
            rows, cols = place(u, a)
            (j, count), (_, size) = units[u]
            s3[u, a].wait_recv()
            total = part[rows, b1, b2, keep, cols] + r3[rows, :, cols]
            at = pl.ds(j * piece, count * piece)
            wg_ref[at, cols] = total.reshape(count * piece, size // 2)
            store(wg_ref.at[at, cols], wg_hbm.at[at, cols])

    def local_grads(h):
        at = columns(h)
        fq32, fk32 = features(r["q"][:, at]), features(r["k"][:, at])
        v = r["v"][:, at]
        dn = r["da"][at, :]
        dden = r["dd"][pl.ds(h, 1), :]
        mask = causal()
        scores = jnp.where(mask, dot(r["fk"][:, at], r["fq"][:, at], NT), 0.0)
        dp = jnp.where(mask, mm(v, dn, NN) + dden, 0.0)
        z = jnp.broadcast_to(r["vae"][pl.ds(h, 1), :], (8, HEAD))
        top = lax.broadcasted_iota(jnp.int32, (8, tokens), 0) == 0
        left = jnp.concatenate([dn, jnp.where(top, dden, 0.0)], axis=0)
        right = jnp.concatenate([state.entry(at), z], axis=0)
        dfq = mm(dp, fk32, TN) + mm(left, right, TN)
        dq_ref[:, at] = (dfq * jnp.minimum(fq32, 1.0)).astype(BF)
        dfk = mm(dp, fq32, NN)
        for i in range(tokens // HEAD):
            r["nl"][at, pl.ds(i * HEAD, HEAD)] = dfk[i * HEAD:(i + 1) * HEAD, :]
        r["dvl"][:, at] = mm(scores, dn, NT)

    def later_grads(h):
        at = columns(h)
        fk32 = features(r["k"][:, at])
        g = grad.entry(at)
        dfk = jnp.concatenate([r["nl"][at, pl.ds(i * HEAD, HEAD)] for i in range(tokens // HEAD)], axis=0)
        dfk = dfk + mm(r["v"][:, at], g, NN) + r["vbe"][pl.ds(h, 1), :]
        dk_ref[:, at] = (dfk * jnp.minimum(fk32, 1.0)).astype(BF)
        dv_ref[:, at] = (r["dvl"][:, at] + mm(fk32, g, NT)).astype(BF)

    def early(start, stop):
        loop(start, stop, 2, local_grads)
        at = pl.ds(start * HEAD, (stop - start) * HEAD)
        store(dq_ref.at[:, at], dq_hbm.at[:, at])

    def late(start, stop):
        loop(start, stop, 2, later_grads)
        at = pl.ds(start * HEAD, (stop - start) * HEAD)
        store(dk_ref.at[:, at], dk_hbm.at[:, at])
        store(dv_ref.at[:, at], dv_hbm.at[:, at])

    early(0, 2)
    take(3)
    gather(0)
    pass_on(2)
    multiply(0)
    first(0)
    grad.settle()
    zgrad.climb()
    relay(4)
    early(2, 4)
    gather(1)
    pass_on(3)
    multiply(1)
    first(1)
    grad.join()
    zgrad.finish()
    relay(5)
    gather(2)
    offer(6)
    share(6)
    multiply(2)
    second(0)
    first(2)
    early(4, 6)
    gather(3)
    offer(7)
    share(7)
    multiply(3)
    second(1)
    third(0)
    first(3)
    grad.finish()
    early(6, 8)
    take(4, 5)
    multiply(4)
    second(2)
    third(1)
    first(4)
    last(0)
    early(8, 10)
    relay(6)
    multiply(5)
    second(3)
    third(2)
    first(5)
    last(1)
    early(10, 12)
    relay(7)
    take(6, 7)
    multiply(6)
    second(4)
    third(3)
    first(6)
    last(2)
    early(12, 14)
    multiply(7)
    second(5)
    third(4)
    first(7)
    last(3)
    early(14, 16)
    late(0, 4)
    second(6)
    third(5)
    last(4)
    late(4, 8)
    second(7)
    third(6)
    last(5)
    late(8, 12)
    third(7)
    last(6)
    late(12, 16)
    last(7)
    for made in stores:
        made.wait()
    links.drain()


def hand_over(count, *refs):
    ins, outs, held, sem = refs[:count], refs[count:2 * count], refs[2 * count:3 * count], refs[3 * count]
    moves = []
    for i in range(count):
        rows = ins[i].shape[0] // PIECES
        for j in range(PIECES):
            at = pl.ds(j * rows, rows)
            n = len(moves)
            moves.append((pltpu.make_async_copy(ins[i].at[at], held[i].at[at], sem.at[2 * n]),
                          pltpu.make_async_copy(held[i].at[at], outs[i].at[at], sem.at[2 * n + 1])))
    for first, _ in moves:
        first.start()
    for first, second in moves:
        first.wait()
        second.start()
    for _, second in moves:
        second.wait()


def body(queries, keys, values, out_weight, out_grad):
    assert lax.axis_size("seq") == 32
    tokens, width = queries.shape
    out_width = out_grad.shape[1]
    vm = scratch_of(tokens, width, out_width)
    like = jax.ShapeDtypeStruct
    anywhere = pl.BlockSpec(memory_space=pl.ANY)
    dma = pltpu.SemaphoreType.DMA
    made = pl.pallas_call(
        functools.partial(kernel, list(vm)),
        out_shape=[like(queries.shape, BF)] * 3 + [like((width // 32, out_width), F32)],
        in_specs=[anywhere] * 5,
        out_specs=[pl.BlockSpec(memory_space=pltpu.HBM)] * 4,
        scratch_shapes=[pltpu.VMEM(shape, kind) for shape, kind in vm.values()]
        + [dma((4,)), dma((W_SLOTS,)), dma((COPIES,)), dma((COPIES,)), dma((48,))],
        compiler_params=pltpu.CompilerParams(collective_id=0, has_side_effects=True, vmem_limit_bytes=58 << 20),
        cost_estimate=pl.CostEstimate(flops=10_000_000_000, bytes_accessed=16_000_000, transcendentals=0),
    )(queries, keys, values, out_weight, out_grad)
    return pl.pallas_call(
        functools.partial(hand_over, len(made)),
        out_shape=[like(x.shape, x.dtype) for x in made],
        in_specs=[pl.BlockSpec(memory_space=pltpu.HBM)] * len(made),
        out_specs=[pl.BlockSpec(memory_space=pltpu.HBM)] * len(made),
        scratch_shapes=[pltpu.VMEM(x.shape, x.dtype) for x in made] + [dma((2 * PIECES * len(made),))],
        compiler_params=pltpu.CompilerParams(vmem_limit_bytes=60 << 20),
    )(*made)


def solution(mesh):
    rows = P(("groups", "seq"), None)
    return jax.shard_map(
        lambda *args: tuple(body(*args)), mesh=mesh, in_specs=(rows, rows, rows, P(), rows),
        out_specs=(rows, rows, rows, rows), check_vma=False)
```
